256 devices in a mesh: blk: 16 (over z, x_lo), head: 4 (over x_hi, core), batch: 4 (over y).
Axes of the slice: x: 4 (x_hi: 2, x_lo: 2; x = x_hi * 2 + x_lo), y: 4, z: 8, core: 2. Of those that a mesh axis runs over, the one named last changes fastest.
Arguments:
- query_rows: bfloat16 [16384, 3072], P(('batch', 'blk'), 'head'), parts along dimension 0, may hold values from -6 to 6
- key_rows: bfloat16 [16384, 3072], P(('batch', 'blk'), 'head'), parts along dimension 0, may hold values from -6 to 6
- value_rows: bfloat16 [16384, 3072], P(('batch', 'blk'), 'head'), parts along dimension 0, may hold values from -6 to 6
- query_tangent: bfloat16 [16384, 3072], P(('batch', 'blk'), 'head'), parts along dimension 0, may hold values from -6 to 6
- key_tangent: bfloat16 [16384, 3072], P(('batch', 'blk'), 'head'), parts along dimension 0, may hold values from -6 to 6
- value_tangent: bfloat16 [16384, 3072], P(('batch', 'blk'), 'head'), parts along dimension 0, may hold values from -6 to 6
Outputs:
- attended: bfloat16 [16384, 3072], P(('batch', 'blk', 'head')), parts along dimension 0
- attended_tangent: bfloat16 [16384, 3072], P(('batch', 'blk', 'head')), parts along dimension 0
The draws below stay inside these ranges and needn't reach their ends.
There are 4 independent parts, one for each index of `batch`. The reference program is written for one: setup_inputs(seed, part) draws one part's arguments, and reference() takes and returns one part's arrays. A program takes and returns all parts, laid end to end along the dimension named above; each array names one. Nothing has to cross between parts.
All inputs are finite; a program needn't handle non-finite values.
Results may differ from the reference program's by a relative error of at most 0.011.
Values may be sent and summed in bfloat16 or wider, within the bound.
A program may use at most 128 MiB of HBM per device.

```python
import math
import jax
import jax.numpy as jnp
from jax import lax

HEADS = 24
HD = 128
TOKENS = 4096
WIDTH = 3072


def rough_rows(key, lowest, highest):
    noise_key, factor_key = jax.random.split(key)
    noise_table = jax.random.normal(noise_key, (TOKENS, WIDTH), jnp.float32)
    factors = jnp.exp(jax.random.uniform(factor_key, (TOKENS, 1), jnp.float32, math.log(lowest), math.log(highest)))
    return jnp.clip(noise_table * factors, -6.0, 6.0)


def draw_query_rows(key, part):
    drawn = rough_rows(jax.random.fold_in(key, 11), 0.5, 2.5)
    return drawn.astype(jnp.bfloat16)


def draw_key_rows(key, part):
    drawn = rough_rows(jax.random.fold_in(key, 13), 1.0, 1.2)
    return drawn.astype(jnp.bfloat16)


def block_levels(rng, dims, cuts, low, high):
    factor_of = 1.0
    for axis_at, blocks in cuts:
        steps = jax.random.uniform(jax.random.fold_in(jax.random.fold_in(rng, 6), axis_at), (blocks,), jnp.float32, low / len(cuts), high / len(cuts))
        factor_of = factor_of * jnp.repeat(jnp.exp(steps), dims[axis_at] // blocks).reshape((-1,) + (1,) * (len(dims) - 1 - axis_at))
    return factor_of


def bell_draw(stream_key, dims, scale, limit, pieces=(), kind=jnp.bfloat16):
    gain = block_levels(stream_key, dims, pieces, -0.22, 0.18) if pieces else 1.0
    array = jax.random.normal(stream_key, dims, jnp.float32) * scale * gain
    return jnp.minimum(jnp.maximum(array, -limit), limit).astype(kind)


def setup_inputs(seed: int = 0, part: int = 0) -> dict:
    streams_of = jax.random.split(jax.random.key(seed), 7)
    part_keys = jax.random.split(jax.random.fold_in(streams_of[6], part), 7)
    return {
        "query_rows": draw_query_rows(jax.random.fold_in(jax.random.fold_in(streams_of[6], part), 71), part),
        "key_rows": draw_key_rows(jax.random.fold_in(jax.random.fold_in(streams_of[6], part), 71), part),
        "value_rows": bell_draw(part_keys[2], (TOKENS, WIDTH), 1.0, 6.0, ((0, 16), (1, 4))),
        "query_tangent": bell_draw(part_keys[3], (TOKENS, WIDTH), 1.0, 6.0, ((0, 16), (1, 4))),
        "key_tangent": bell_draw(part_keys[4], (TOKENS, WIDTH), 1.0, 6.0, ((0, 16), (1, 4))),
        "value_tangent": bell_draw(part_keys[5], (TOKENS, WIDTH), 1.0, 6.0, ((0, 16), (1, 4))),
    }


def one_head(members):
    query_part, key_part, value_part, query_change, key_change, value_change = members
    scaling = HD ** -0.5
    scores = jnp.dot(query_part, key_part.T, preferred_element_type=jnp.float32) * scaling
    score_change = (jnp.dot(query_change, key_part.T, preferred_element_type=jnp.float32)
                    + jnp.dot(query_part, key_change.T, preferred_element_type=jnp.float32)) * scaling
    row_max = jnp.max(scores, axis=1, keepdims=True)
    weights = jnp.exp(scores - row_max)
    mixed_terms = weights * score_change
    row_total = jnp.sum(weights, axis=1, keepdims=True)
    row_shift = jnp.sum(mixed_terms, axis=1, keepdims=True)
    weights_low = weights.astype(jnp.bfloat16)
    mixed_low = mixed_terms.astype(jnp.bfloat16)
    numerator = jnp.dot(weights_low, value_part, preferred_element_type=jnp.float32)
    tangent_numerator = (jnp.dot(mixed_low, value_part, preferred_element_type=jnp.float32)
                         + jnp.dot(weights_low, value_change, preferred_element_type=jnp.float32))
    attended = numerator / row_total
    attended_tangent = tangent_numerator / row_total - (row_shift / row_total) * attended
    return attended.astype(jnp.bfloat16), attended_tangent.astype(jnp.bfloat16)


def by_head(matrix):
    return matrix.reshape(TOKENS, HEADS, HD).transpose(1, 0, 2)


def back_rows(stacked):
    return stacked.transpose(1, 0, 2).reshape(TOKENS, HEADS * HD)


def reference(query_rows, key_rows, value_rows, query_tangent, key_tangent, value_tangent):
    members = (by_head(query_rows), by_head(key_rows), by_head(value_rows),
               by_head(query_tangent), by_head(key_tangent), by_head(value_tangent))
    attended, attended_tangent = lax.map(one_head, members)
    return back_rows(attended), back_rows(attended_tangent)
```

```python
import functools

import jax
import jax.numpy as jnp
from jax import lax
from jax.experimental import pallas as pl
from jax.experimental.pallas import tpu as pltpu
from jax.sharding import PartitionSpec as P

HD = 128
MESH = pl.DeviceIdType.MESH
LOWEST = -1e30
LOG2E = 1.4426950408889634
NT = (((1,), (1,)), ((), ()))

NZ = 8
OWN = 6


def owner_z(i, column):
    return lax.rem(i + i // 3 + 2 * column, NZ)


def kernel(
    rows, q_in, k_in, v_in, qt_in, kt_in, vt_in, o_ref, ot_ref,
    qq, kk, vv, acc, acct, top, total, shift, res,
    send_in, got_q, got_k, got_v, pass_k, pass_v, come_k, come_v, send_out, got_out,
):
    quarter = rows // 4
    blk, head, y = lax.axis_index("blk"), lax.axis_index("head"), lax.axis_index("batch")
    z, s = blk // 2, lax.rem(blk, 2)
    x_hi, core = head // 2, lax.rem(head, 2)
    place = lax.rem(z + NZ - 2 * s, NZ)
    active = lax.rem(place, 4) != 3
    mine = place - place // 4
    at_home = jnp.logical_and(active, s == core)

    def device(to_blk, to_head):
        return (to_blk, to_head, y)

    barrier = pltpu.get_barrier_semaphore()

    def greet(to_blk, to_head):
        pl.semaphore_signal(barrier, inc=1, device_id=device(to_blk, to_head), device_id_type=MESH)

    @pl.when(active)
    def _():
        greet(blk, 2 * x_hi + 1 - core)

        @pl.loop(0, NZ)
        def _(j):
            @pl.when(jnp.logical_not(jnp.logical_and(j == z, s == core)))
            def _():
                greet(2 * j + core, 2 * x_hi + s)

    @pl.loop(0, OWN)
    def _(i):
        for column in range(2):
            for half in range(2):
                zo = owner_z(i, column)
                to_blk, to_head = 2 * zo + column, 2 * half + s

                @pl.when(jnp.logical_not(jnp.logical_and(to_blk == blk, to_head == head)))
                def _():
                    greet(to_blk, to_head)

    expected = jnp.where(active, OWN + 1 + 32, OWN) - jnp.where(at_home, 2, 0)
    pl.semaphore_wait(barrier, expected)

    def each_owner(act):
        @pl.loop(0, OWN)
        def _(n):
            i = lax.rem(n + z, OWN)
            act(i, owner_z(i, core))

    def send(i, zo, a, src_ref, dst_ref, got):
        src = src_ref.at[:, pl.ds(pl.multiple_of(i * HD, HD), HD)]
        here = jnp.logical_and(zo == z, s == core)

        @pl.when(here)
        def _():
            pltpu.make_async_copy(src, dst_ref, got).start()

        @pl.when(jnp.logical_not(here))
        def _():
            pltpu.make_async_remote_copy(
                src_ref=src, dst_ref=dst_ref, send_sem=send_in.at[a, i], recv_sem=got,
                device_id=device(2 * zo + core, 2 * x_hi + s), device_id_type=MESH,
            ).start()

    def send_queries(i, zo):
        send(i, zo, 0, qt_in, qq.at[z, :, 0:HD], got_q.at[z])
        send(i, zo, 1, q_in, qq.at[z, :, HD:2 * HD], got_q.at[z])

    def send_keys(i, zo):
        send(i, zo, 2, k_in, kk.at[s, z, :, 0:HD], got_k.at[z])
        send(i, zo, 3, kt_in, kk.at[s, z, :, HD:2 * HD], got_k.at[z])
        send(i, zo, 4, v_in, vv.at[s, z, :, 0:HD], got_v.at[z])
        send(i, zo, 5, vt_in, vv.at[s, z, :, HD:2 * HD], got_v.at[z])

    each_owner(send_queries)
    each_owner(send_keys)

    scaling = HD ** -0.5
    factor = scaling * LOG2E

    def attend(j, kb, vb):
        at = pl.ds(pl.multiple_of(j * rows, rows), rows)
        both = qq[j]
        keys = kb[...]
        scores = lax.dot_general(both[:, HD:], keys[:, :HD], NT, preferred_element_type=jnp.float32)
        change = lax.dot_general(both, keys, NT, preferred_element_type=jnp.float32)
        old = top[at, :]
        new = jnp.maximum(old, jnp.max(scores, axis=1, keepdims=True))
        shrink = jnp.exp2((old - new) * factor)
        weights = jnp.exp2((scores - new[:, :1]) * factor)
        mixed = weights * change
        top[at, :] = new
        total[at, :] = total[at, :] * shrink + jnp.sum(weights, axis=1, keepdims=True)
        shift[at, :] = shift[at, :] * shrink + jnp.sum(mixed, axis=1, keepdims=True)
        values = vb[...]
        shrinks = jnp.concatenate([shrink, shrink], axis=1)
        acc[at, :] = acc[at, :] * shrinks + jnp.dot(
            weights.astype(jnp.bfloat16), values, preferred_element_type=jnp.float32)
        acct[at, :] = acct[at, :] * shrink + jnp.dot(
            mixed.astype(jnp.bfloat16), values[:, :HD], preferred_element_type=jnp.float32)

    def to_sibling(j, src, send_sem, recv_sem):
        return pltpu.make_async_remote_copy(
            src_ref=src.at[core, j], dst_ref=src.at[core, j], send_sem=send_sem.at[j], recv_sem=recv_sem.at[j],
            device_id=device(blk, 2 * x_hi + 1 - core), device_id_type=MESH,
        )

    def landed(ref, sem):
        pltpu.make_async_copy(ref, ref, sem).wait()

    column0 = (2 * x_hi + s) * OWN + mine
    out_columns = pl.ds(pl.multiple_of(column0 * HD, HD), HD)

    def send_result(j):
        for part in range(4):
            piece = pl.ds(pl.multiple_of(j * rows + part * quarter, quarter), quarter)
            here = jnp.logical_and(2 * j + core == blk, head == part)
            for a, out in ((0, o_ref), (1, ot_ref)):
                src = res.at[a, piece, :]
                dst = out.at[:, out_columns]

                @pl.when(here)
                def _():
                    pltpu.make_async_copy(src, dst, got_out.at[a]).start()

                @pl.when(jnp.logical_not(here))
                def _():
                    pltpu.make_async_remote_copy(
                        src_ref=src, dst_ref=dst, send_sem=send_out.at[a, j, part], recv_sem=got_out.at[a],
                        device_id=device(2 * j + core, part), device_id_type=MESH,
                    ).start()

    def finish(j):
        at = pl.ds(pl.multiple_of(j * rows, rows), rows)
        inverse = 1.0 / total[at, :]
        attended = acc[at, 0:HD] * inverse
        tangent = (acct[at, :] * scaling + acc[at, HD:2 * HD]) * inverse
        tangent = tangent - (shift[at, :] * scaling * inverse) * attended
        res[0, at, :] = attended.astype(jnp.bfloat16)
        res[1, at, :] = tangent.astype(jnp.bfloat16)

    @pl.when(active)
    def _():
        top[...] = jnp.full_like(top, LOWEST)
        total[...] = jnp.zeros_like(total)
        shift[...] = jnp.zeros_like(shift)
        acc[...] = jnp.zeros_like(acc)
        acct[...] = jnp.zeros_like(acct)

        @pl.loop(0, NZ)
        def _(j):
            landed(qq.at[j], got_q.at[j])

        @pl.loop(0, NZ)
        def _(n):
            b = lax.rem(z + n, NZ)
            landed(kk.at[core, b], got_k.at[b])
            to_sibling(b, kk, pass_k, come_k).start()
            landed(vv.at[core, b], got_v.at[b])
            to_sibling(b, vv, pass_v, come_v).start()

            @pl.loop(0, NZ)
            def _(j):
                attend(j, kk.at[core, b], vv.at[core, b])

            landed(kk.at[1 - core, b], come_k.at[b])
            landed(vv.at[1 - core, b], come_v.at[b])

            @pl.loop(0, NZ)
            def _(m):
                j = lax.rem(m + z, NZ)
                attend(j, kk.at[1 - core, b], vv.at[1 - core, b])

                @pl.when(n == NZ - 1)
                def _():
                    finish(j)
                    send_result(j)

    def sent(i, zo):
        @pl.when(jnp.logical_not(jnp.logical_and(zo == z, s == core)))
        def _():
            for a, src_ref in enumerate((qt_in, q_in, k_in, kt_in, v_in, vt_in)):
                src = src_ref.at[:, pl.ds(pl.multiple_of(i * HD, HD), HD)]
                pltpu.make_async_copy(src, src, send_in.at[a, i]).wait()

    each_owner(sent)

    @pl.when(active)
    def _():
        @pl.loop(0, NZ)
        def _(j):
            landed(kk.at[core, j], pass_k.at[j])
            landed(vv.at[core, j], pass_v.at[j])
            for part in range(4):
                piece = pl.ds(pl.multiple_of(j * rows + part * quarter, quarter), quarter)

                @pl.when(jnp.logical_not(jnp.logical_and(2 * j + core == blk, head == part)))
                def _():
                    for a in range(2):
                        landed(res.at[a, piece, :], send_out.at[a, j, part])

    landed(o_ref, got_out.at[0])
    landed(ot_ref, got_out.at[1])


def local(*arrays):
    rows = arrays[0].shape[0]
    out = jax.ShapeDtypeStruct((rows // 4, 24 * HD), jnp.bfloat16)
    queries = NZ * rows
    f32 = jnp.float32
    dma = pltpu.SemaphoreType.DMA
    return tuple(pl.pallas_call(
        functools.partial(kernel, rows),
        out_shape=(out, out),
        in_specs=[pl.BlockSpec(memory_space=pl.ANY)] * 6,
        out_specs=(pl.BlockSpec(memory_space=pltpu.VMEM),) * 2,
        scratch_shapes=[
            pltpu.VMEM((NZ, rows, 2 * HD), jnp.bfloat16),
            pltpu.VMEM((2, NZ, rows, 2 * HD), jnp.bfloat16),
            pltpu.VMEM((2, NZ, rows, 2 * HD), jnp.bfloat16),
            pltpu.VMEM((queries, 2 * HD), f32),
            pltpu.VMEM((queries, HD), f32),
            pltpu.VMEM((queries, HD), f32),
            pltpu.VMEM((queries, HD), f32),
            pltpu.VMEM((queries, HD), f32),
            pltpu.VMEM((2, queries, HD), jnp.bfloat16),
            dma((6, OWN)), dma((NZ,)), dma((NZ,)), dma((NZ,)),
            dma((NZ,)), dma((NZ,)), dma((NZ,)), dma((NZ,)),
            dma((2, NZ, 4)), dma((2,)),
        ],
        compiler_params=pltpu.CompilerParams(
            collective_id=0, has_side_effects=True, vmem_limit_bytes=48 * 2**20),
        name="attention_tangent",
    )(*arrays))


def solution(mesh):
    rows_in = P(("batch", "blk"), "head")
    rows_out = P(("batch", "blk", "head"), None)
    return jax.shard_map(
        local, mesh=mesh, in_specs=(rows_in,) * 6, out_specs=(rows_out, rows_out), check_vma=False,
    )
```

```python
import functools

import jax
import jax.numpy as jnp
from jax import lax
from jax.experimental import pallas as pl
from jax.experimental.pallas import tpu as pltpu
from jax.sharding import PartitionSpec as P

HD = 128
MESH = pl.DeviceIdType.MESH
LOG2E = 1.4426950408889634
NT = (((1,), (1,)), ((), ()))

NZ = 8
MANY = 2048
OWN = 6


def step_of(n, turn):
    away = (3 - (n - 2) // 2) * (1 - 2 * (n % 2))
    return turn * (0 if n == 0 else 4 if n == 1 else away)


def step_at(n, turn):
    away = (3 - (n - 2) // 2) * (1 - 2 * lax.rem(n, 2))
    return turn * jnp.where(n == 0, 0, jnp.where(n == 1, 4, away))


def kernel(
    rows, q_in, k_in, v_in, qt_in, kt_in, vt_in, o_ref, ot_ref,
    qq, kk, vv, res, got,
    send_in, got_q, got_k, got_v, pass_k, pass_v, come_k, come_v, send_out, got_out,
):
    quarter = rows // 4
    blk, head, y = lax.axis_index("blk"), lax.axis_index("head"), lax.axis_index("batch")
    z, s = blk // 2, lax.rem(blk, 2)
    x_hi, core = head // 2, lax.rem(head, 2)
    place = lax.rem(z + NZ - 2 * s, NZ)
    active = lax.rem(place, 4) != 3
    mine = place - place // 4
    at_home = jnp.logical_and(active, s == core)

    def device(to_blk, to_head):
        return (to_blk, to_head, y)

    barrier = pltpu.get_barrier_semaphore()

    def greet(to_blk, to_head):
        pl.semaphore_signal(barrier, inc=1, device_id=device(to_blk, to_head), device_id_type=MESH)

    @pl.when(active)
    def _():
        @pl.loop(0, NZ)
        def _(j):
            @pl.when(jnp.logical_not(jnp.logical_and(j == z, s == core)))
            def _():
                greet(2 * j + core, 2 * x_hi + s)

    for other in range(1, 4):
        greet(blk, lax.rem(head + other, 4))
    pl.semaphore_wait(barrier, OWN + 3 - jnp.where(at_home, 1, 0))

    sources = (qt_in, q_in, k_in, kt_in, v_in, vt_in)
    turn = 1 - 2 * core

    def owner_at(n):
        zo = lax.rem(z + step_of(n, turn) + NZ, NZ)
        there = lax.rem(zo + NZ - 2 * core, NZ)
        return zo, there - there // 4, lax.rem(there, 4) != 3

    def slot(n, side):
        return pl.ds(pl.multiple_of((2 * n + side) * rows, rows), rows)

    def send(n, a):
        zo, i, owns = owner_at(n)
        src = sources[a].at[:, pl.ds(pl.multiple_of(i * HD, HD), HD)]
        half = slice(HD * (a % 2), HD * (a % 2 + 1))
        if a < 2:
            dst, got_sem = qq.at[n * rows:(n + 1) * rows, half], got_q.at[n]
        elif a < 4:
            dst, got_sem = kk.at[slot(n, s), half], got_k.at[n]
        else:
            dst, got_sem = vv.at[slot(n, s), half], got_v.at[n]

        def local():
            pltpu.make_async_copy(src, dst, got_sem).start()

        def remote():
            pltpu.make_async_remote_copy(
                src_ref=src, dst_ref=dst, send_sem=send_in.at[a, i], recv_sem=got_sem,
                device_id=device(2 * zo + core, 2 * x_hi + s), device_id_type=MESH,
            ).start()

        if n == 0:
            pl.when(jnp.logical_and(owns, s == core))(local)
            pl.when(jnp.logical_and(owns, s != core))(remote)
        else:
            pl.when(owns)(remote)

    for kinds, steps in (((0, 1), (0,)), ((2, 3, 4, 5), (0, 2, 4, 6)), ((0, 1), (2, 4, 6))):
        for n in steps:
            for a in kinds:
                send(n, a)
                send(n + 1, a)

    scaling = HD ** -0.5
    factor = scaling * LOG2E

    def wide(a, count):
        return jnp.concatenate([a] * count, axis=1)

    def lanes(a):
        parts = [a[:, c:c + HD] for c in range(0, a.shape[1], HD)]
        return functools.reduce(jnp.add, parts)

    def attend(n):
        both = qq[pl.ds(pl.multiple_of(n * rows, rows), rows), :]
        count = NZ * 2 * rows
        part = min(count, MANY)
        for c in range(0, count, part):
            keys, values = kk[c:c + part, :], vv[c:c + part, :]
            scores = lax.dot_general(both[:, HD:], keys[:, :HD], NT, preferred_element_type=jnp.float32)
            change = lax.dot_general(both, keys, NT, preferred_element_type=jnp.float32)
            peak = jnp.broadcast_to(jnp.max(scores, axis=1, keepdims=True), (rows, HD))
            new = peak if c == 0 else jnp.maximum(top, peak)
            weights = jnp.exp2((scores - wide(new, part // HD)) * factor)
            mixed = weights * change
            sums = lanes(weights), lanes(mixed)
            mix = jnp.dot(weights.astype(jnp.bfloat16), values, preferred_element_type=jnp.float32)
            mixt = jnp.dot(mixed.astype(jnp.bfloat16), values[:, :HD], preferred_element_type=jnp.float32)
            if c == 0:
                top, total, shift, acc, acct = new, *sums, mix, mixt
            else:
                shrink = jnp.exp2((top - new) * factor)
                top, total, shift = new, total * shrink + sums[0], shift * shrink + sums[1]
                acc, acct = acc * wide(shrink, 2) + mix, acct * shrink + mixt
        inverse = 1.0 / jnp.sum(total, axis=1, keepdims=True)
        shifted = jnp.sum(shift, axis=1, keepdims=True) * (scaling * inverse)
        attended = acc[:, :HD] * inverse
        tangent = (acct * scaling + acc[:, HD:]) * inverse - shifted * attended
        for a, result in ((0, attended), (1, tangent)):
            for p in range(4):
                res[n, p, a] = result[p * quarter:(p + 1) * quarter, :].astype(jnp.bfloat16)

    def to_sibling(n, ref, send_sem, recv_sem):
        mine = ref.at[slot(n, core), :]
        return pltpu.make_async_remote_copy(
            src_ref=mine, dst_ref=mine, send_sem=send_sem.at[n], recv_sem=recv_sem.at[n],
            device_id=device(blk, 2 * x_hi + 1 - core), device_id_type=MESH,
        )

    def landed(ref, sem):
        pltpu.make_async_copy(ref, ref, sem).wait()

    column0 = (2 * x_hi + s) * OWN + mine

    def row_home(n):
        return 2 * lax.rem(z - step_at(n, 1 - 2 * s) + NZ, NZ) + core

    def send_result(n):
        home = row_home(n)
        for part in range(4):
            src, dst = res.at[n, part], got.at[column0]
            here = jnp.logical_and(home == blk, head == part)

            @pl.when(here)
            def _():
                pltpu.make_async_copy(src, dst, got_out).start()

            @pl.when(jnp.logical_not(here))
            def _():
                pltpu.make_async_remote_copy(
                    src_ref=src, dst_ref=dst, send_sem=send_out.at[n, part], recv_sem=got_out,
                    device_id=device(home, part), device_id_type=MESH,
                ).start()

    @pl.when(active)
    def _():
        @pl.loop(0, NZ)
        def _(n):
            landed(kk.at[slot(n, core), :], got_k.at[n])
            to_sibling(n, kk, pass_k, come_k).start()
            landed(vv.at[slot(n, core), :], got_v.at[n])
            to_sibling(n, vv, pass_v, come_v).start()

        @pl.loop(0, NZ)
        def _(n):
            landed(kk.at[slot(n, 1 - core), :], come_k.at[n])
            landed(vv.at[slot(n, 1 - core), :], come_v.at[n])

        @pl.loop(0, NZ)
        def _(n):
            landed(qq.at[pl.ds(pl.multiple_of(n * rows, rows), rows), :], got_q.at[n])
            attend(n)
            send_result(n)

    for n in range(NZ):
        zo, i, owns = owner_at(n)
        src = q_in.at[:, pl.ds(pl.multiple_of(i * HD, HD), HD)]

        @pl.when(jnp.logical_and(owns, s != core) if n == 0 else owns)
        def _():
            for a in range(6):
                landed(src, send_in.at[a, i])

    @pl.when(active)
    def _():
        @pl.loop(0, NZ)
        def _(n):
            landed(kk.at[slot(n, core), :], pass_k.at[n])
            landed(vv.at[slot(n, core), :], pass_v.at[n])
            for part in range(4):
                @pl.when(jnp.logical_not(jnp.logical_and(row_home(n) == blk, head == part)))
                def _():
                    landed(res.at[n, part], send_out.at[n, part])

    landed(got, got_out)
    for h in range(4 * OWN):
        o_ref[:, h * HD:(h + 1) * HD] = got[h, 0]
        ot_ref[:, h * HD:(h + 1) * HD] = got[h, 1]


def local(*arrays):
    rows = arrays[0].shape[0]
    out = jax.ShapeDtypeStruct((rows // 4, 24 * HD), jnp.bfloat16)
    queries = NZ * rows
    bf16 = jnp.bfloat16
    dma = pltpu.SemaphoreType.DMA
    return tuple(pl.pallas_call(
        functools.partial(kernel, rows),
        out_shape=(out, out),
        in_specs=[pl.BlockSpec(memory_space=pltpu.HBM)] * 6,
        out_specs=(pl.BlockSpec(memory_space=pltpu.VMEM),) * 2,
        scratch_shapes=[
            pltpu.VMEM((queries, 2 * HD), bf16),
            pltpu.VMEM((2 * queries, 2 * HD), bf16),
            pltpu.VMEM((2 * queries, 2 * HD), bf16),
            pltpu.VMEM((NZ, 4, 2, rows // 4, HD), bf16),
            pltpu.VMEM((4 * OWN, 2, rows // 4, HD), bf16),
            dma((6, OWN)), dma((NZ,)), dma((NZ,)), dma((NZ,)),
            dma((NZ,)), dma((NZ,)), dma((NZ,)), dma((NZ,)),
            dma((NZ, 4)), dma,
        ],
        compiler_params=pltpu.CompilerParams(
            collective_id=0, has_side_effects=True, vmem_limit_bytes=62 * 2**20),
        name="attention_tangent",
    )(*arrays))


def solution(mesh):
    rows_in = P(("batch", "blk"), "head")
    rows_out = P(("batch", "blk", "head"), None)
    return jax.shard_map(
        local, mesh=mesh, in_specs=(rows_in,) * 6, out_specs=(rows_out, rows_out), check_vma=False,
    )
```

```python
import functools

import jax
import jax.numpy as jnp
from jax import lax
from jax.experimental import pallas as pl
from jax.experimental.pallas import tpu as pltpu
from jax.sharding import PartitionSpec as P

HD = 128
MESH = pl.DeviceIdType.MESH
LOG2E = 1.4426950408889634
NT = (((1,), (1,)), ((), ()))

NZ = 8
QUERIES, KEYS = (0, 1), (2, 3, 4, 5)
RELAYED = (0, 2, 3)
MANY = 2048
OWN = 6


def step_of(n, turn):
    away = (3 - (n - 2) // 2) * (1 - 2 * (n % 2))
    return turn * (0 if n == 0 else 4 if n == 1 else away)


def step_at(n, turn):
    away = (3 - (n - 2) // 2) * (1 - 2 * lax.rem(n, 2))
    return turn * jnp.where(n == 0, 0, jnp.where(n == 1, 4, away))


def kernel(
    rows, q_in, k_in, v_in, qt_in, kt_in, vt_in, got,
    qq, kk, vv, res, relay,
    send_in, got_q, got_k, got_v, pass_k, pass_v, come_k, come_v, send_out, got_out, relay_in, relay_out,
):
    quarter = rows // 4
    blk, head, y = lax.axis_index("blk"), lax.axis_index("head"), lax.axis_index("batch")
    z, s = blk // 2, lax.rem(blk, 2)
    x_hi, core = head // 2, lax.rem(head, 2)
    place = lax.rem(z + NZ - 2 * s, NZ)
    active = lax.rem(place, 4) != 3
    mine = place - place // 4
    at_home = jnp.logical_and(active, s == core)

    def device(to_blk, to_head):
        return (to_blk, to_head, y)

    barrier = pltpu.get_barrier_semaphore()

    def greet(to_blk, to_head):
        pl.semaphore_signal(barrier, inc=1, device_id=device(to_blk, to_head), device_id_type=MESH)

    @pl.when(active)
    def _():
        @pl.loop(0, NZ)
        def _(j):
            @pl.when(jnp.logical_not(jnp.logical_and(j == z, s == core)))
            def _():
                greet(2 * j + core, 2 * x_hi + s)

    for other in range(1, 4):
        greet(blk, lax.rem(head + other, 4))
    partner = lax.rem(z + 2 * lax.rem(z, 2) + NZ - 1, NZ)
    greet(2 * partner + s, head)
    pl.semaphore_wait(barrier, OWN + 4 - jnp.where(at_home, 1, 0))

    sources = (qt_in, q_in, k_in, kt_in, v_in, vt_in)
    turn = 1 - 2 * core

    def owner_at(n):
        return owner_on(lax.rem(z + step_of(n, turn) + NZ, NZ))

    def owner_on(zo):
        there = lax.rem(zo + NZ - 2 * core, NZ)
        return zo, there - there // 4, lax.rem(there, 4) != 3

    def slot(n, side):
        return pl.ds(pl.multiple_of((2 * n + side) * rows, rows), rows)

    def place_of(n, a):
        half = slice(HD * (a % 2), HD * (a % 2 + 1))
        if a < 2:
            return qq.at[n * rows:(n + 1) * rows, half], got_q.at[n]
        if a < 4:
            return kk.at[slot(n, s), half], got_k.at[n]
        return vv.at[slot(n, s), half], got_v.at[n]

    def send(n, a):
        zo, i, owns = owner_at(n)
        src = sources[a].at[:, pl.ds(pl.multiple_of(i * HD, HD), HD)]
        dst, got_sem = place_of(n, a)
        to = device(2 * zo + core, 2 * x_hi + s)
        if n == 1 and a in RELAYED:
            r = RELAYED.index(a)
            dst, got_sem, to = relay.at[r], relay_in.at[r], device(2 * partner + s, head)

        def local():
            pltpu.make_async_copy(src, dst, got_sem).start()

        def remote():
            pltpu.make_async_remote_copy(
                src_ref=src, dst_ref=dst, send_sem=send_in.at[a, i], recv_sem=got_sem,
                device_id=to, device_id_type=MESH,
            ).start()

        if n == 0:
            pl.when(jnp.logical_and(owns, s == core))(local)
            pl.when(jnp.logical_and(owns, s != core))(remote)
        else:
            pl.when(owns)(remote)

    def send_all(kinds, steps):
        for n in steps:
            for a in kinds:
                send(n, a)
                send(n + 1, a)

    def sent(kinds):
        for n in range(NZ):
            zo, i, owns = owner_at(n)
            src = q_in.at[:, pl.ds(pl.multiple_of(i * HD, HD), HD)]

            @pl.when(jnp.logical_and(owns, s != core) if n == 0 else owns)
            def _():
                for a in kinds:
                    pltpu.make_async_copy(src, src, send_in.at[a, i]).wait()

    send_all(QUERIES, (0,))
    send_all(KEYS, (0, 2, 4, 6))

    zo_partner, _, relays = owner_on(lax.rem(partner + NZ // 2, NZ))

    def pass_on(r):
        dst, got_sem = place_of(1, RELAYED[r])
        return pltpu.make_async_remote_copy(
            src_ref=relay.at[r], dst_ref=dst, send_sem=relay_out.at[r], recv_sem=got_sem,
            device_id=device(2 * zo_partner + core, 2 * x_hi + s), device_id_type=MESH,
        )

    @pl.when(relays)
    def _():
        for r in range(len(RELAYED)):
            pltpu.make_async_copy(relay.at[r], relay.at[r], relay_in.at[r]).wait()
            pass_on(r).start()

    @pl.when(jnp.logical_not(active))
    def _():
        sent(KEYS)
        send_all(QUERIES, (2, 4, 6))

    scaling = HD ** -0.5
    factor = scaling * LOG2E

    def wide(a, count):
        return jnp.concatenate([a] * count, axis=1)

    def lanes(a):
        parts = [a[:, c:c + HD] for c in range(0, a.shape[1], HD)]
        return functools.reduce(jnp.add, parts)

    def attend(n):
        both = qq[pl.ds(pl.multiple_of(n * rows, rows), rows), :]
        count = NZ * 2 * rows
        part = min(count, MANY)
        for c in range(0, count, part):
            keys, values = kk[c:c + part, :], vv[c:c + part, :]
            scores = lax.dot_general(both[:, HD:], keys[:, :HD], NT, preferred_element_type=jnp.float32)
            change = lax.dot_general(both, keys, NT, preferred_element_type=jnp.float32)
            peak = jnp.broadcast_to(jnp.max(scores, axis=1, keepdims=True), (rows, HD))
            new = peak if c == 0 else jnp.maximum(top, peak)
            weights = jnp.exp2((scores - wide(new, part // HD)) * factor)
            mixed = weights * change
            sums = lanes(weights), lanes(mixed)
            mix = jnp.dot(weights.astype(jnp.bfloat16), values, preferred_element_type=jnp.float32)
            mixt = jnp.dot(mixed.astype(jnp.bfloat16), values[:, :HD], preferred_element_type=jnp.float32)
            if c == 0:
                top, total, shift, acc, acct = new, *sums, mix, mixt
            else:
                shrink = jnp.exp2((top - new) * factor)
                top, total, shift = new, total * shrink + sums[0], shift * shrink + sums[1]
                acc, acct = acc * wide(shrink, 2) + mix, acct * shrink + mixt
        inverse = 1.0 / jnp.sum(total, axis=1, keepdims=True)
        shifted = jnp.sum(shift, axis=1, keepdims=True) * (scaling * inverse)
        attended = acc[:, :HD] * inverse
        tangent = (acct * scaling + acc[:, HD:]) * inverse - shifted * attended
        for a, result in ((0, attended), (1, tangent)):
            for p in range(4):
                res[n, p, a] = result[p * quarter:(p + 1) * quarter, :].astype(jnp.bfloat16)

    def to_sibling(n, ref, send_sem, recv_sem):
        mine = ref.at[slot(n, core), :]
        return pltpu.make_async_remote_copy(
            src_ref=mine, dst_ref=mine, send_sem=send_sem.at[n], recv_sem=recv_sem.at[n],
            device_id=device(blk, 2 * x_hi + 1 - core), device_id_type=MESH,
        )

    def landed(ref, sem):
        pltpu.make_async_copy(ref, ref, sem).wait()

    column0 = (2 * x_hi + s) * OWN + mine

    def row_home(n):
        return 2 * lax.rem(z - step_at(n, 1 - 2 * s) + NZ, NZ) + core

    def send_result(n):
        home = row_home(n)
        for part in range(4):
            src, dst = res.at[n, part], got.at[column0]
            here = jnp.logical_and(home == blk, head == part)

            @pl.when(here)
            def _():
                pltpu.make_async_copy(src, dst, got_out).start()

            @pl.when(jnp.logical_not(here))
            def _():
                pltpu.make_async_remote_copy(
                    src_ref=src, dst_ref=dst, send_sem=send_out.at[n, part], recv_sem=got_out,
                    device_id=device(home, part), device_id_type=MESH,
                ).start()

    @pl.when(active)
    def _():
        @pl.loop(0, NZ)
        def _(n):
            landed(kk.at[slot(n, core), :], got_k.at[n])
            to_sibling(n, kk, pass_k, come_k).start()
            landed(vv.at[slot(n, core), :], got_v.at[n])
            to_sibling(n, vv, pass_v, come_v).start()

        send_all(QUERIES, (2, 4, 6))

        @pl.loop(0, NZ)
        def _(n):
            landed(kk.at[slot(n, 1 - core), :], come_k.at[n])
            landed(vv.at[slot(n, 1 - core), :], come_v.at[n])

        @pl.loop(0, NZ)
        def _(n):
            landed(qq.at[pl.ds(pl.multiple_of(n * rows, rows), rows), :], got_q.at[n])
            attend(n)
            send_result(n)

    sent(QUERIES)

    @pl.when(relays)
    def _():
        for r in range(len(RELAYED)):
            pass_on(r).wait_send()

    @pl.when(active)
    def _():
        sent(KEYS)

        @pl.loop(0, NZ)
        def _(n):
            landed(kk.at[slot(n, core), :], pass_k.at[n])
            landed(vv.at[slot(n, core), :], pass_v.at[n])
            for part in range(4):
                @pl.when(jnp.logical_not(jnp.logical_and(row_home(n) == blk, head == part)))
                def _():
                    landed(res.at[n, part], send_out.at[n, part])

    landed(got, got_out)


def local(*arrays):
    rows = arrays[0].shape[0]
    queries = NZ * rows
    bf16 = jnp.bfloat16
    dma = pltpu.SemaphoreType.DMA
    got = pl.pallas_call(
        functools.partial(kernel, rows),
        out_shape=jax.ShapeDtypeStruct((4 * OWN, 2, rows // 4, HD), bf16),
        in_specs=[pl.BlockSpec(memory_space=pltpu.HBM)] * 6,
        out_specs=pl.BlockSpec(memory_space=pltpu.HBM),
        scratch_shapes=[
            pltpu.VMEM((queries, 2 * HD), bf16),
            pltpu.VMEM((2 * queries, 2 * HD), bf16),
            pltpu.VMEM((2 * queries, 2 * HD), bf16),
            pltpu.VMEM((NZ, 4, 2, rows // 4, HD), bf16),
            pltpu.VMEM((len(RELAYED), rows, HD), bf16),
            dma((6, OWN)), dma((NZ,)), dma((NZ,)), dma((NZ,)),
            dma((NZ,)), dma((NZ,)), dma((NZ,)), dma((NZ,)),
            dma((NZ, 4)), dma, dma((len(RELAYED),)), dma((len(RELAYED),)),
        ],
        compiler_params=pltpu.CompilerParams(
            collective_id=0, has_side_effects=True, vmem_limit_bytes=62 * 2**20),
        name="attention_tangent",
    )(*arrays)
    return tuple(got[:, a].transpose(1, 0, 2).reshape(rows // 4, -1) for a in range(2))


def solution(mesh):
    rows_in = P(("batch", "blk"), "head")
    rows_out = P(("batch", "blk", "head"), None)
    return jax.shard_map(
        local, mesh=mesh, in_specs=(rows_in,) * 6, out_specs=(rows_out, rows_out), check_vma=False,
    )
```

```python
import functools

import jax
import jax.numpy as jnp
from jax import lax
from jax.experimental import pallas as pl
from jax.experimental.pallas import tpu as pltpu
from jax.sharding import PartitionSpec as P

HD = 128
MESH = pl.DeviceIdType.MESH
LOG2E = 1.4426950408889634
NT = (((1,), (1,)), ((), ()))

NZ = 8
QUERIES, KEYS = (0, 1), (2, 3, 4, 5)
EARLY, LATE = ((0,), (1,)), ((2, 3), (4, 5), (6, 7))
RELAYED = (0, 2, 3)
MANY = 2048
OWN = 6


def step_of(n, turn):
    away = (3 - (n - 2) // 2) * (1 - 2 * (n % 2))
    return turn * (0 if n == 0 else 4 if n == 1 else away)


def step_at(n, turn):
    away = (3 - (n - 2) // 2) * (1 - 2 * lax.rem(n, 2))
    return turn * jnp.where(n == 0, 0, jnp.where(n == 1, 4, away))


def kernel(
    rows, q_in, k_in, v_in, qt_in, kt_in, vt_in, got,
    qq, kk, vv, res, relay,
    send_in, got_q, got_k, got_v, pass_k, pass_v, come_k, come_v, send_out, got_out, relay_in, relay_out,
):
    quarter = rows // 4
    blk, head, y = lax.axis_index("blk"), lax.axis_index("head"), lax.axis_index("batch")
    z, s = blk // 2, lax.rem(blk, 2)
    x_hi, core = head // 2, lax.rem(head, 2)
    place = lax.rem(z + NZ - 2 * s, NZ)
    active = lax.rem(place, 4) != 3
    mine = place - place // 4
    at_home = jnp.logical_and(active, s == core)

    def device(to_blk, to_head):
        return (to_blk, to_head, y)

    barrier = pltpu.get_barrier_semaphore()

    def greet(to_blk, to_head):
        pl.semaphore_signal(barrier, inc=1, device_id=device(to_blk, to_head), device_id_type=MESH)

    @pl.when(active)
    def _():
        @pl.loop(0, NZ)
        def _(j):
            @pl.when(jnp.logical_not(jnp.logical_and(j == z, s == core)))
            def _():
                greet(2 * j + core, 2 * x_hi + s)

    for other in range(1, 4):
        greet(blk, lax.rem(head + other, 4))
    partner = lax.rem(z + 2 * lax.rem(z, 2) + NZ - 1, NZ)
    greet(2 * partner + s, head)
    pl.semaphore_wait(barrier, OWN + 4 - jnp.where(at_home, 1, 0))

    sources = (qt_in, q_in, k_in, kt_in, v_in, vt_in)
    turn = 1 - 2 * core

    def owner_at(n):
        return owner_on(lax.rem(z + step_of(n, turn) + NZ, NZ))

    def owner_on(zo):
        there = lax.rem(zo + NZ - 2 * core, NZ)
        return zo, there - there // 4, lax.rem(there, 4) != 3

    def slot(n, side):
        return pl.ds(pl.multiple_of((2 * n + side) * rows, rows), rows)

    def place_of(n, a):
        half = slice(HD * (a % 2), HD * (a % 2 + 1))
        if a < 2:
            return qq.at[n * rows:(n + 1) * rows, half], got_q.at[n]
        if a < 4:
            return kk.at[slot(n, s), half], got_k.at[n]
        return vv.at[slot(n, s), half], got_v.at[n]

    def send(n, a):
        zo, i, owns = owner_at(n)
        src = sources[a].at[:, pl.ds(pl.multiple_of(i * HD, HD), HD)]
        dst, got_sem = place_of(n, a)
        to = device(2 * zo + core, 2 * x_hi + s)
        if n == 1 and a in RELAYED:
            r = RELAYED.index(a)
            dst, got_sem, to = relay.at[r], relay_in.at[r], device(2 * partner + s, head)

        def local():
            pltpu.make_async_copy(src, dst, got_sem).start()

        def remote():
            pltpu.make_async_remote_copy(
                src_ref=src, dst_ref=dst, send_sem=send_in.at[a, i], recv_sem=got_sem,
                device_id=to, device_id_type=MESH,
            ).start()

        if n == 0:
            pl.when(jnp.logical_and(owns, s == core))(local)
            pl.when(jnp.logical_and(owns, s != core))(remote)
        else:
            pl.when(owns)(remote)

    def send_all(kinds, steps):
        for some in steps:
            for a in kinds:
                for n in some:
                    send(n, a)

    def sent(kinds):
        for n in range(NZ):
            zo, i, owns = owner_at(n)
            src = q_in.at[:, pl.ds(pl.multiple_of(i * HD, HD), HD)]

            @pl.when(jnp.logical_and(owns, s != core) if n == 0 else owns)
            def _():
                for a in kinds:
                    pltpu.make_async_copy(src, src, send_in.at[a, i]).wait()

    send_all(QUERIES, EARLY)
    send_all(KEYS, ((0, 1), (2, 3), (4, 5), (6, 7)))

    zo_partner, _, relays = owner_on(lax.rem(partner + NZ // 2, NZ))

    def pass_on(r):
        dst, got_sem = place_of(1, RELAYED[r])
        return pltpu.make_async_remote_copy(
            src_ref=relay.at[r], dst_ref=dst, send_sem=relay_out.at[r], recv_sem=got_sem,
            device_id=device(2 * zo_partner + core, 2 * x_hi + s), device_id_type=MESH,
        )

    def relay_all(kinds):
        @pl.when(relays)
        def _():
            for r, a in enumerate(RELAYED):
                if a in kinds:
                    pltpu.make_async_copy(relay.at[r], relay.at[r], relay_in.at[r]).wait()
                    pass_on(r).start()

    relay_all(QUERIES + KEYS)

    @pl.when(jnp.logical_not(active))
    def _():
        sent(KEYS)
        send_all(QUERIES, LATE)


    scaling = HD ** -0.5
    factor = scaling * LOG2E

    def wide(a, count):
        return jnp.concatenate([a] * count, axis=1)

    def lanes(a):
        parts = [a[:, c:c + HD] for c in range(0, a.shape[1], HD)]
        return functools.reduce(jnp.add, parts)

    def attend(n):
        both = qq[pl.ds(pl.multiple_of(n * rows, rows), rows), :]
        count = NZ * 2 * rows
        part = min(count, MANY)
        for c in range(0, count, part):
            keys, values = kk[c:c + part, :], vv[c:c + part, :]
            scores = lax.dot_general(both[:, HD:], keys[:, :HD], NT, preferred_element_type=jnp.float32)
            change = lax.dot_general(both, keys, NT, preferred_element_type=jnp.float32)
            peak = jnp.broadcast_to(jnp.max(scores, axis=1, keepdims=True), (rows, HD))
            new = peak if c == 0 else jnp.maximum(top, peak)
            weights = jnp.exp2((scores - wide(new, part // HD)) * factor)
            mixed = weights * change
            sums = lanes(weights), lanes(mixed)
            mix = jnp.dot(weights.astype(jnp.bfloat16), values, preferred_element_type=jnp.float32)
            mixt = jnp.dot(mixed.astype(jnp.bfloat16), values[:, :HD], preferred_element_type=jnp.float32)
            if c == 0:
                top, total, shift, acc, acct = new, *sums, mix, mixt
            else:
                shrink = jnp.exp2((top - new) * factor)
                top, total, shift = new, total * shrink + sums[0], shift * shrink + sums[1]
                acc, acct = acc * wide(shrink, 2) + mix, acct * shrink + mixt
        inverse = 1.0 / jnp.sum(total, axis=1, keepdims=True)
        shifted = jnp.sum(shift, axis=1, keepdims=True) * (scaling * inverse)
        attended = acc[:, :HD] * inverse
        tangent = (acct * scaling + acc[:, HD:]) * inverse - shifted * attended
        for a, result in ((0, attended), (1, tangent)):
            for p in range(4):
                res[n, p, a] = result[p * quarter:(p + 1) * quarter, :].astype(jnp.bfloat16)

    def to_sibling(n, ref, send_sem, recv_sem):
        mine = ref.at[slot(n, core), :]
        return pltpu.make_async_remote_copy(
            src_ref=mine, dst_ref=mine, send_sem=send_sem.at[n], recv_sem=recv_sem.at[n],
            device_id=device(blk, 2 * x_hi + 1 - core), device_id_type=MESH,
        )

    def landed(ref, sem):
        pltpu.make_async_copy(ref, ref, sem).wait()

    columns = pl.ds(pl.multiple_of(((2 * x_hi + s) * OWN + mine) * HD, HD), HD)

    def row_home(n):
        return 2 * lax.rem(z - step_at(n, 1 - 2 * s) + NZ, NZ) + core

    def send_result(n):
        home = row_home(n)
        for part in range(4):
            src, dst = res.at[n, part], got.at[:, :, columns]
            here = jnp.logical_and(home == blk, head == part)

            @pl.when(here)
            def _():
                pltpu.make_async_copy(src, dst, got_out).start()

            @pl.when(jnp.logical_not(here))
            def _():
                pltpu.make_async_remote_copy(
                    src_ref=src, dst_ref=dst, send_sem=send_out.at[n, part], recv_sem=got_out,
                    device_id=device(home, part), device_id_type=MESH,
                ).start()

    @pl.when(active)
    def _():
        def arrive(n):
            landed(kk.at[slot(n, core), :], got_k.at[n])
            to_sibling(n, kk, pass_k, come_k).start()
            landed(vv.at[slot(n, core), :], got_v.at[n])
            to_sibling(n, vv, pass_v, come_v).start()

        pl.loop(0, 5)(arrive)
        send_all(QUERIES, LATE)
        pl.loop(5, NZ)(arrive)

        @pl.loop(0, NZ)
        def _(n):
            landed(kk.at[slot(n, 1 - core), :], come_k.at[n])
            landed(vv.at[slot(n, 1 - core), :], come_v.at[n])

        @pl.loop(0, NZ)
        def _(n):
            landed(qq.at[pl.ds(pl.multiple_of(n * rows, rows), rows), :], got_q.at[n])
            attend(n)
            send_result(n)

    sent(QUERIES)

    @pl.when(relays)
    def _():
        for r in range(len(RELAYED)):
            pass_on(r).wait_send()

    @pl.when(active)
    def _():
        sent(KEYS)

        @pl.loop(0, NZ)
        def _(n):
            landed(kk.at[slot(n, core), :], pass_k.at[n])
            landed(vv.at[slot(n, core), :], pass_v.at[n])
            for part in range(4):
                @pl.when(jnp.logical_not(jnp.logical_and(row_home(n) == blk, head == part)))
                def _():
                    landed(res.at[n, part], send_out.at[n, part])

    landed(got, got_out)


def local(*arrays):
    rows = arrays[0].shape[0]
    queries = NZ * rows
    bf16 = jnp.bfloat16
    dma = pltpu.SemaphoreType.DMA
    got = pl.pallas_call(
        functools.partial(kernel, rows),
        out_shape=jax.ShapeDtypeStruct((2, rows // 4, 4 * OWN * HD), bf16),
        in_specs=[pl.BlockSpec(memory_space=pltpu.HBM)] * 6,
        out_specs=pl.BlockSpec(memory_space=pltpu.HBM),
        scratch_shapes=[
            pltpu.VMEM((queries, 2 * HD), bf16),
            pltpu.VMEM((2 * queries, 2 * HD), bf16),
            pltpu.VMEM((2 * queries, 2 * HD), bf16),
            pltpu.VMEM((NZ, 4, 2, rows // 4, HD), bf16),
            pltpu.VMEM((len(RELAYED), rows, HD), bf16),
            dma((6, OWN)), dma((NZ,)), dma((NZ,)), dma((NZ,)),
            dma((NZ,)), dma((NZ,)), dma((NZ,)), dma((NZ,)),
            dma((NZ, 4)), dma, dma((len(RELAYED),)), dma((len(RELAYED),)),
        ],
        compiler_params=pltpu.CompilerParams(
            collective_id=0, has_side_effects=True, vmem_limit_bytes=62 * 2**20),
        name="attention_tangent",
    )(*arrays)
    return got[0], got[1]


def solution(mesh):
    rows_in = P(("batch", "blk"), "head")
    rows_out = P(("batch", "blk", "head"), None)
    return jax.shard_map(
        local, mesh=mesh, in_specs=(rows_in,) * 6, out_specs=(rows_out, rows_out), check_vma=False,
    )
```

```python
import functools

import jax
import jax.numpy as jnp
from jax import lax
from jax.experimental import pallas as pl
from jax.experimental.pallas import tpu as pltpu
from jax.sharding import PartitionSpec as P

HD = 128
MESH = pl.DeviceIdType.MESH
LOG2E = 1.4426950408889634
NT = (((1,), (1,)), ((), ()))

NZ = 8
QUERIES, KEYS = (0, 1), (2, 3, 4, 5)
EARLY, LATE = ((0,), (1,)), ((2, 3), (4, 5), (6, 7))
RELAYED = (0, 2, 3)
MANY = 2048
OWN = 6


def step_of(n, turn):
    away = (3 - (n - 2) // 2) * (1 - 2 * (n % 2))
    return turn * (0 if n == 0 else 4 if n == 1 else away)


def step_at(n, turn):
    away = (3 - (n - 2) // 2) * (1 - 2 * lax.rem(n, 2))
    return turn * jnp.where(n == 0, 0, jnp.where(n == 1, 4, away))


def kernel(
    rows, q_in, k_in, v_in, qt_in, kt_in, vt_in, got,
    qq, kk, vv, res, relay,
    send_in, got_q, got_k, got_v, pass_k, pass_v, come_k, come_v, send_out, got_out, relay_in, relay_out,
):
    quarter = rows // 4
    blk, head, y = lax.axis_index("blk"), lax.axis_index("head"), lax.axis_index("batch")
    z, s = blk // 2, lax.rem(blk, 2)
    x_hi, core = head // 2, lax.rem(head, 2)
    place = lax.rem(z + NZ - 2 * s, NZ)
    active = lax.rem(place, 4) != 3
    mine = place - place // 4
    at_home = jnp.logical_and(active, s == core)

    def device(to_blk, to_head):
        return (to_blk, to_head, y)

    barrier = pltpu.get_barrier_semaphore()

    def greet(to_blk, to_head):
        pl.semaphore_signal(barrier, inc=1, device_id=device(to_blk, to_head), device_id_type=MESH)

    @pl.when(active)
    def _():
        @pl.loop(0, NZ)
        def _(j):
            @pl.when(jnp.logical_not(jnp.logical_and(j == z, s == core)))
            def _():
                greet(2 * j + core, 2 * x_hi + s)

    for other in range(1, 4):
        greet(blk, lax.rem(head + other, 4))
    partner = lax.rem(z + 2 * lax.rem(z, 2) + NZ - 1, NZ)
    greet(2 * partner + s, head)
    pl.semaphore_wait(barrier, OWN + 4 - jnp.where(at_home, 1, 0))

    sources = (qt_in, q_in, k_in, kt_in, v_in, vt_in)
    turn = 1 - 2 * core

    def owner_at(n):
        return owner_on(lax.rem(z + step_of(n, turn) + NZ, NZ))

    def owner_on(zo):
        there = lax.rem(zo + NZ - 2 * core, NZ)
        return zo, there - there // 4, lax.rem(there, 4) != 3

    def slot(n, side):
        return pl.ds(pl.multiple_of((2 * n + side) * rows, rows), rows)

    def place_of(n, a):
        half = slice(HD * (a % 2), HD * (a % 2 + 1))
        if a < 2:
            return qq.at[n * rows:(n + 1) * rows, half], got_q.at[n]
        if a < 4:
            return kk.at[slot(n, s), half], got_k.at[n]
        return vv.at[slot(n, s), half], got_v.at[n]

    def send(n, a):
        zo, i, owns = owner_at(n)
        src = sources[a].at[:, pl.ds(pl.multiple_of(i * HD, HD), HD)]
        dst, got_sem = place_of(n, a)
        to = device(2 * zo + core, 2 * x_hi + s)
        if n == 1 and a in RELAYED:
            r = RELAYED.index(a)
            dst, got_sem, to = relay.at[r], relay_in.at[r], device(2 * partner + s, head)

        def local():
            pltpu.make_async_copy(src, dst, got_sem).start()

        def remote():
            pltpu.make_async_remote_copy(
                src_ref=src, dst_ref=dst, send_sem=send_in.at[a, i], recv_sem=got_sem,
                device_id=to, device_id_type=MESH,
            ).start()

        if n == 0:
            pl.when(jnp.logical_and(owns, s == core))(local)
            pl.when(jnp.logical_and(owns, s != core))(remote)
        else:
            pl.when(owns)(remote)

    def send_all(kinds, steps):
        for some in steps:
            for a in kinds:
                for n in some:
                    send(n, a)

    def sent(kinds, steps=range(NZ)):
        for n in steps:
            zo, i, owns = owner_at(n)
            src = q_in.at[:, pl.ds(pl.multiple_of(i * HD, HD), HD)]

            @pl.when(jnp.logical_and(owns, s != core) if n == 0 else owns)
            def _():
                for a in kinds:
                    pltpu.make_async_copy(src, src, send_in.at[a, i]).wait()

    send_all(QUERIES, EARLY)
    send_all(KEYS, ((0, 1), (2, 3), (4, 5), (6, 7)))

    zo_partner, _, relays = owner_on(lax.rem(partner + NZ // 2, NZ))

    def pass_on(r):
        dst, got_sem = place_of(1, RELAYED[r])
        return pltpu.make_async_remote_copy(
            src_ref=relay.at[r], dst_ref=dst, send_sem=relay_out.at[r], recv_sem=got_sem,
            device_id=device(2 * zo_partner + core, 2 * x_hi + s), device_id_type=MESH,
        )

    def relay_all(kinds):
        @pl.when(relays)
        def _():
            for r, a in enumerate(RELAYED):
                if a in kinds:
                    pltpu.make_async_copy(relay.at[r], relay.at[r], relay_in.at[r]).wait()
                    pass_on(r).start()

    relay_all(QUERIES + KEYS)

    @pl.when(jnp.logical_not(active))
    def _():
        sent(KEYS)
        for some in LATE:
            send_all(QUERIES, (some,))
            sent(QUERIES, some)

    scaling = HD ** -0.5
    factor = scaling * LOG2E

    def wide(a, count):
        return jnp.concatenate([a] * count, axis=1)

    def lanes(a):
        parts = [a[:, c:c + HD] for c in range(0, a.shape[1], HD)]
        return functools.reduce(jnp.add, parts)

    def attend(n):
        both = qq[pl.ds(pl.multiple_of(n * rows, rows), rows), :]
        count = NZ * 2 * rows
        part = min(count, MANY)
        for c in range(0, count, part):
            keys, values = kk[c:c + part, :], vv[c:c + part, :]
            scores = lax.dot_general(both[:, HD:], keys[:, :HD], NT, preferred_element_type=jnp.float32)
            change = lax.dot_general(both, keys, NT, preferred_element_type=jnp.float32)
            peak = jnp.broadcast_to(jnp.max(scores, axis=1, keepdims=True), (rows, HD))
            new = peak if c == 0 else jnp.maximum(top, peak)
            weights = jnp.exp2((scores - wide(new, part // HD)) * factor)
            mixed = weights * change
            sums = lanes(weights), lanes(mixed)
            mix = jnp.dot(weights.astype(jnp.bfloat16), values, preferred_element_type=jnp.float32)
            mixt = jnp.dot(mixed.astype(jnp.bfloat16), values[:, :HD], preferred_element_type=jnp.float32)
            if c == 0:
                top, total, shift, acc, acct = new, *sums, mix, mixt
            else:
                shrink = jnp.exp2((top - new) * factor)
                top, total, shift = new, total * shrink + sums[0], shift * shrink + sums[1]
                acc, acct = acc * wide(shrink, 2) + mix, acct * shrink + mixt
        inverse = 1.0 / jnp.sum(total, axis=1, keepdims=True)
        shifted = jnp.sum(shift, axis=1, keepdims=True) * (scaling * inverse)
        attended = acc[:, :HD] * inverse
        tangent = (acct * scaling + acc[:, HD:]) * inverse - shifted * attended
        for a, result in ((0, attended), (1, tangent)):
            for p in range(4):
                res[n, p, a] = result[p * quarter:(p + 1) * quarter, :].astype(jnp.bfloat16)

    def to_sibling(n, ref, send_sem, recv_sem):
        mine = ref.at[slot(n, core), :]
        return pltpu.make_async_remote_copy(
            src_ref=mine, dst_ref=mine, send_sem=send_sem.at[n], recv_sem=recv_sem.at[n],
            device_id=device(blk, 2 * x_hi + 1 - core), device_id_type=MESH,
        )

    def landed(ref, sem):
        pltpu.make_async_copy(ref, ref, sem).wait()

    columns = pl.ds(pl.multiple_of(((2 * x_hi + s) * OWN + mine) * HD, HD), HD)

    def row_home(n):
        return 2 * lax.rem(z - step_at(n, 1 - 2 * s) + NZ, NZ) + core

    def send_result(n):
        home = row_home(n)
        for part in range(4):
            src, dst = res.at[n, part], got.at[:, :, columns]
            here = jnp.logical_and(home == blk, head == part)

            @pl.when(here)
            def _():
                pltpu.make_async_copy(src, dst, got_out).start()

            @pl.when(jnp.logical_not(here))
            def _():
                pltpu.make_async_remote_copy(
                    src_ref=src, dst_ref=dst, send_sem=send_out.at[n, part], recv_sem=got_out,
                    device_id=device(home, part), device_id_type=MESH,
                ).start()

    @pl.when(active)
    def _():
        def arrive(n):
            landed(kk.at[slot(n, core), :], got_k.at[n])
            to_sibling(n, kk, pass_k, come_k).start()
            landed(vv.at[slot(n, core), :], got_v.at[n])
            to_sibling(n, vv, pass_v, come_v).start()

        pl.loop(0, 7)(arrive)
        send_all(QUERIES, LATE[:1])
        pl.loop(7, NZ)(arrive)

        @pl.loop(0, NZ)
        def _(n):
            landed(kk.at[slot(n, 1 - core), :], come_k.at[n])
            landed(vv.at[slot(n, 1 - core), :], come_v.at[n])

        @pl.loop(0, NZ)
        def _(n):
            for k in range(1, len(LATE)):
                pl.when(n == 2 * k - 2)(functools.partial(send_all, QUERIES, (LATE[k],)))
            landed(qq.at[pl.ds(pl.multiple_of(n * rows, rows), rows), :], got_q.at[n])
            attend(n)
            send_result(n)

    pl.when(active)(lambda: sent(QUERIES))
    pl.when(jnp.logical_not(active))(lambda: sent(QUERIES, sum(EARLY, ())))

    @pl.when(relays)
    def _():
        for r in range(len(RELAYED)):
            pass_on(r).wait_send()

    @pl.when(active)
    def _():
        sent(KEYS)

        @pl.loop(0, NZ)
        def _(n):
            landed(kk.at[slot(n, core), :], pass_k.at[n])
            landed(vv.at[slot(n, core), :], pass_v.at[n])
            for part in range(4):
                @pl.when(jnp.logical_not(jnp.logical_and(row_home(n) == blk, head == part)))
                def _():
                    landed(res.at[n, part], send_out.at[n, part])

    landed(got, got_out)


def local(*arrays):
    rows = arrays[0].shape[0]
    queries = NZ * rows
    bf16 = jnp.bfloat16
    dma = pltpu.SemaphoreType.DMA
    got = pl.pallas_call(
        functools.partial(kernel, rows),
        out_shape=jax.ShapeDtypeStruct((2, rows // 4, 4 * OWN * HD), bf16),
        in_specs=[pl.BlockSpec(memory_space=pltpu.HBM)] * 6,
        out_specs=pl.BlockSpec(memory_space=pltpu.HBM),
        scratch_shapes=[
            pltpu.VMEM((queries, 2 * HD), bf16),
            pltpu.VMEM((2 * queries, 2 * HD), bf16),
            pltpu.VMEM((2 * queries, 2 * HD), bf16),
            pltpu.VMEM((NZ, 4, 2, rows // 4, HD), bf16),
            pltpu.VMEM((len(RELAYED), rows, HD), bf16),
            dma((6, OWN)), dma((NZ,)), dma((NZ,)), dma((NZ,)),
            dma((NZ,)), dma((NZ,)), dma((NZ,)), dma((NZ,)),
            dma((NZ, 4)), dma, dma((len(RELAYED),)), dma((len(RELAYED),)),
        ],
        compiler_params=pltpu.CompilerParams(
            collective_id=0, has_side_effects=True, vmem_limit_bytes=62 * 2**20),
        name="attention_tangent",
    )(*arrays)
    return got[0], got[1]


def solution(mesh):
    rows_in = P(("batch", "blk"), "head")
    rows_out = P(("batch", "blk", "head"), None)
    return jax.shard_map(
        local, mesh=mesh, in_specs=(rows_in,) * 6, out_specs=(rows_out, rows_out), check_vma=False,
    )
```
